256 devices in a mesh: req: 32 (over x, z), kv: 8 (over y, core).
Axes of the slice: x: 4, y: 4, z: 8, core: 2. Of those that a mesh axis runs over, the one named last changes fastest.
Arguments:
- hidden: bfloat16 [128, 5120], P('kv', 'req'), may hold values from -120 to 120
- gain: bfloat16 [5120], P('req'), may hold values from 0.5 to 1.5
- w_query: bfloat16 [5120, 5120], P('req', 'kv'), may hold values from -0.078125 to 0.078125
- w_key: bfloat16 [5120, 1024], P('req', 'kv'), may hold values from -0.078125 to 0.078125
- w_value: bfloat16 [5120, 1024], P('req', 'kv'), may hold values from -0.078125 to 0.078125
- b_query: bfloat16 [5120], P('kv'), may hold values from -3 to 3
- b_key: bfloat16 [1024], P('kv'), may hold values from -3 to 3
- b_value: bfloat16 [1024], P('kv'), may hold values from -3 to 3
- w_output: bfloat16 [5120, 5120], P('kv', 'req'), may hold values from -0.5 to 0.5
- key_cache: bfloat16 [128, 8, 4096, 128], P('req', 'kv'), may hold values from -160 to 160
- value_cache: bfloat16 [128, 8, 4096, 128], P('req', 'kv'), may hold values from -9 to 9
- sink_keys: bfloat16 [128, 8, 4, 128], P('req', 'kv'), may hold values from -6 to 6
- sink_values: bfloat16 [128, 8, 4, 128], P('req', 'kv'), may hold values from -9 to 9
- lengths: int32 [128], P('req'), may hold values from 4 to 8192, as said below
- sink_count: int32 [128], P('req'), may hold values from 0 to 4, as said below
- window: int32 [128], P('req'), may hold values from 1024 to 4096, as said below
Outputs:
- attn_out: bfloat16 [128, 5120], P('kv', 'req')
The draws below stay inside these ranges and needn't reach their ends.
Inputs may be any that keep to these rules, and one draw needn't show every extreme that they name: `lengths`: exactly 8 requests have length 8192; the others are heavy-tailed below it. `sink_count`: some request keeps 4. Some request has window 4096.
All inputs are finite; a program needn't handle non-finite values.
Results may differ from the reference program's by a relative error of at most 0.012.
The reference program's roundings to bfloat16 on the way count: a program that leaves them out, or rounds other values in their place, can miss the bound.
Values may be sent and summed in bfloat16 or wider, within the bound.
A program may use at most 64 MiB of HBM per device.

```python
import math
import jax
import jax.numpy as jnp
from jax import lax

D = 5120
HQ = 40
KVH = 8
HD = 128
GROUP = 5
REQUESTS = 128
CYCLE = 4096
SINKS = 4
MAXLEN = 8192
LONGS = 8


def draw_hidden(key, part):
    first = jax.random.fold_in(key, 0)
    ramp = jnp.exp(math.log(3.0) * jnp.arange(D, dtype=jnp.float32) / D)
    base = jnp.clip(jax.random.normal(first, (REQUESTS, D), jnp.float32), -4.0, 4.0)
    return (base * ramp[None, :]).astype(jnp.bfloat16)


def draw_key_cache(key, part):
    first = jax.random.fold_in(key, 0)
    shape = (REQUESTS, KVH, CYCLE, HD)
    base = jnp.clip(jax.random.normal(first, shape, jnp.float32), -5.0, 5.0)
    return base.astype(jnp.bfloat16)


def draw_lengths(key, part):
    first, second, third = jax.random.split(key, 3)
    top_bit = MAXLEN.bit_length() - 1
    exponent = jax.random.randint(first, (REQUESTS,), 2, top_bit)
    base = jnp.left_shift(jnp.ones((REQUESTS,), jnp.int32), exponent)
    extra = jax.random.randint(second, (REQUESTS,), 0, base)
    result = base + extra
    order = jax.random.permutation(third, REQUESTS)
    return result.at[order[:LONGS]].set(MAXLEN).astype(jnp.int32)


def draw_sink_count(key, part):
    first, second = jax.random.split(jax.random.fold_in(key, 11))
    result = jax.random.randint(first, (REQUESTS,), 0, SINKS + 1)
    where_full = jax.random.randint(second, (), 0, REQUESTS)
    return result.at[where_full].set(SINKS).astype(jnp.int32)


def draw_window(key, part):
    first, second = jax.random.split(jax.random.fold_in(key, 23))
    result = jax.random.randint(first, (REQUESTS,), CYCLE // 4, CYCLE + 1)
    where_full = jax.random.randint(second, (), 0, REQUESTS)
    return result.at[where_full].set(CYCLE).astype(jnp.int32)


def level_of(key, shape, cuts, least, top_value):
    level, own = 1.0, jax.random.fold_in(key, 6)
    for dim, blocks in cuts:
        draws = jnp.exp(jax.random.uniform(jax.random.fold_in(own, dim), (blocks,), jnp.float32, least / len(cuts), top_value / len(cuts)))
        level = level * jnp.repeat(draws, shape[dim] // blocks).reshape([-1 if axis == dim else 1 for axis in range(len(shape))])
    return level


def scatter_about(key, dims, width, most, pieces=(), kind=jnp.bfloat16):
    drawn = jax.random.normal(key, dims, jnp.float32) * width
    if len(pieces) > 0:
        drawn = level_of(key, dims, pieces, -0.22, 0.18) * drawn
    return jnp.clip(drawn, min=-most, max=most).astype(kind)


def setup_inputs(seed: int = 0) -> dict:
    splits = jax.random.split(jax.random.key(seed), 17)
    hidden = draw_hidden(jax.random.fold_in(splits[16], 71), 0)
    gain = jnp.clip(1.0 + 0.1 * jax.random.normal(splits[1], (D,), jnp.float32), 0.5, 1.5).astype(jnp.bfloat16)
    w_query = scatter_about(splits[2], (D, HQ * HD), D ** -0.5, 0.078125, ((0, 32), (1, 8)))
    w_key = scatter_about(splits[3], (D, KVH * HD), D ** -0.5, 0.078125, ((0, 32), (1, 8)))
    w_value = scatter_about(splits[4], (D, KVH * HD), D ** -0.5, 0.078125, ((0, 32), (1, 8)))
    b_query = scatter_about(splits[5], (HQ * HD,), 0.5, 3.0, ((0, 8),))
    b_key = scatter_about(splits[6], (KVH * HD,), 0.5, 3.0, ((0, 8),))
    b_value = scatter_about(splits[7], (KVH * HD,), 0.5, 3.0, ((0, 8),))
    w_output = scatter_about(splits[8], (HQ * HD, D), HD ** -0.5, 0.5, ((0, 8), (1, 32)))
    key_cache = draw_key_cache(jax.random.fold_in(splits[16], 71), 0)
    value_cache = scatter_about(splits[10], (REQUESTS, KVH, CYCLE, HD), 1.5, 9.0, ((0, 32), (1, 8)))
    sink_keys = scatter_about(splits[11], (REQUESTS, KVH, SINKS, HD), 1.0, 6.0, ((0, 32), (1, 8)))
    sink_values = scatter_about(splits[12], (REQUESTS, KVH, SINKS, HD), 1.5, 9.0, ((0, 32), (1, 8)))
    lengths = draw_lengths(jax.random.fold_in(splits[16], 71), 0)
    sink_count = draw_sink_count(jax.random.fold_in(splits[16], 71), 0)
    window = draw_window(jax.random.fold_in(splits[16], 71), 0)
    return {"hidden": hidden, "gain": gain, "w_query": w_query, "w_key": w_key, "w_value": w_value, "b_query": b_query, "b_key": b_key, "b_value": b_value, "w_output": w_output, "key_cache": key_cache, "value_cache": value_cache, "sink_keys": sink_keys, "sink_values": sink_values, "lengths": lengths, "sink_count": sink_count, "window": window}


def rotate(window_values, positions):
    half = window_values.shape[-1] // 2
    freq = jnp.power(1000000.0, -2.0 * jnp.arange(half, dtype=jnp.float32) / window_values.shape[-1])
    angle = positions[..., None] * freq
    cosine = jnp.cos(angle)
    sine = jnp.sin(angle)
    first = window_values[..., :half]
    second = window_values[..., half:]
    return jnp.concatenate([first * cosine - second * sine, second * cosine + first * sine], -1)

def attend(entry_list):
    query_vector, fresh_key, fresh_value, window_keys, window_values, anchor_keys, anchor_values, cache_length, sink_tokens, window = entry_list
    score_scale = 1.0 / math.sqrt(HD)
    query_float = query_vector.astype(jnp.float32)
    s_cache = jnp.einsum('zni,zxi->znx', query_float, window_keys.astype(jnp.float32)) * score_scale
    sink_score = jnp.einsum('zni,zxi->znx', query_float, anchor_keys.astype(jnp.float32)) * score_scale
    s_self = lax.optimization_barrier(jnp.sum(query_float * fresh_key.astype(jnp.float32)[:, None, :], -1)) * score_scale
    slot = jnp.arange(CYCLE, dtype=jnp.int32)
    place = slot + CYCLE * ((cache_length - 1 - slot) // CYCLE)
    live_cache = (slot < cache_length) & (place >= jnp.maximum(sink_tokens, cache_length - window))
    live_sink = jnp.arange(SINKS, dtype=jnp.int32) < jnp.minimum(sink_tokens, cache_length)
    top = jnp.maximum(lax.optimization_barrier(jnp.max(jnp.where(live_cache, s_cache, -jnp.inf), -1)), lax.optimization_barrier(jnp.max(jnp.where(live_sink, sink_score, -jnp.inf), -1)))
    top = jnp.maximum(top, s_self)
    e_cache = jnp.where(live_cache, jnp.exp(s_cache - top[..., None]), 0.0)
    e_sink = jnp.where(live_sink, jnp.exp(sink_score - top[..., None]), 0.0)
    e_self = jnp.exp(s_self - top)
    total = lax.optimization_barrier(jnp.sum(e_cache, -1)) + lax.optimization_barrier(jnp.sum(e_sink, -1)) + e_self
    numer = jnp.einsum('kgs,ksd->kgd', e_cache.astype(jnp.bfloat16).astype(jnp.float32), window_values.astype(jnp.float32))
    numer = numer + jnp.einsum('kgs,ksd->kgd', e_sink.astype(jnp.bfloat16).astype(jnp.float32), anchor_values.astype(jnp.float32))
    numer = numer + e_self.astype(jnp.bfloat16).astype(jnp.float32)[..., None] * fresh_value.astype(jnp.float32)[:, None, :]
    return (numer / total[..., None]).astype(jnp.bfloat16)

def reference(hidden, gain, w_query, w_key, w_value, b_query, b_key, b_value, w_output, key_cache, value_cache, sink_keys, sink_values, lengths, sink_count, window):
    xf = hidden.astype(jnp.float32)
    inv_rms = lax.rsqrt(lax.optimization_barrier(jnp.sum(xf * xf, 1)) / D + 1e-06)
    scaled = (xf * gain.astype(jnp.float32)).astype(jnp.bfloat16)
    query_vector = inv_rms[:, None] * jnp.dot(scaled, w_query, preferred_element_type=jnp.float32) + b_query.astype(jnp.float32)
    fresh_key = inv_rms[:, None] * jnp.dot(scaled, w_key, preferred_element_type=jnp.float32) + b_key.astype(jnp.float32)
    value_f = inv_rms[:, None] * jnp.dot(scaled, w_value, preferred_element_type=jnp.float32) + b_value.astype(jnp.float32)
    positions = lengths.astype(jnp.float32)[:, None]
    q_rot = rotate(query_vector.reshape(REQUESTS, HQ, HD), positions).astype(jnp.bfloat16).reshape(REQUESTS, KVH, GROUP, HD)
    k_rot = rotate(fresh_key.reshape(REQUESTS, KVH, HD), positions).astype(jnp.bfloat16)
    fresh_value = value_f.reshape(REQUESTS, KVH, HD).astype(jnp.bfloat16)
    context = lax.map(attend, (q_rot, k_rot, fresh_value, key_cache, value_cache, sink_keys, sink_values, lengths, sink_count, window))
    context = context.reshape(REQUESTS, HQ * HD)
    return jnp.dot(context, w_output, preferred_element_type=jnp.float32).astype(jnp.bfloat16)
```

```python
import math

import jax
import jax.numpy as jnp
import numpy as np
from jax import lax
from jax.experimental import pallas as pl
from jax.experimental.pallas import tpu as pltpu
from jax.sharding import PartitionSpec as P

D = 5120
CYCLE = 4096
HD = 128
HALF = 64
GROUP = 5
NX, NZ = 4, 8
NREQ, NKV = 32, 8
OWN = 4
ROWS = 16
FEAT = 160
QCOLS = GROUP * HD
MESH = pl.DeviceIdType.MESH
OFFSETS = sorted(
    ((dx, dz) for dx in range(NX) for dz in range(NZ) if (dx, dz) != (0, 0)),
    key=lambda o: -(min(o[0], NX - o[0]) + min(o[1], NZ - o[1])),
)
NT = (((1,), (1,)), ((), ()))


def kernel(
    hid, gain, wq, wk, wv, bq, bk, bv, wo, kc, vc, sk, sv, freq, lens, sinks, wins,
    out,
    hidall, gain_s, w_s, bq_s, bk_s, bv_s, wo_s, k_s, v_s, sk_s, sv_s, freq_s,
    mask_s, emask_s, sinkf_s, bias_s, kext, vext, qs, cs, cb,
    pb, rb, rb2, yb, rb3,
    small_sem, w_sem, k_sem, v_sem, own_sem,
    s1, r1, s2, r2, s4, r4, s5, r5,
):
    r = lax.axis_index("req")
    k = lax.axis_index("kv")
    x, z = r // NZ, lax.rem(r, NZ)

    def peer(o):
        return lax.rem(x + o[0], NX) * NZ + lax.rem(z + o[1], NZ)

    def kv_peer(i):
        return lax.rem(k + i, NKV)

    hid_copy = pltpu.make_async_copy(hid, hidall.at[k], own_sem.at[0])
    hid_copy.start()
    smalls = [
        pltpu.make_async_copy(a, b, small_sem.at[i])
        for i, (a, b) in enumerate(
            [(gain, gain_s), (bq, bq_s), (bk, bk_s), (bv, bv_s), (sk, sk_s), (sv, sv_s), (freq, freq_s)]
        )
    ]
    weights = [
        pltpu.make_async_copy(wq, w_s.at[:, pl.ds(0, QCOLS)], w_sem.at[0]),
        pltpu.make_async_copy(wk, w_s.at[:, pl.ds(QCOLS, HD)], w_sem.at[1]),
        pltpu.make_async_copy(wv, w_s.at[:, pl.ds(QCOLS + HD, HD)], w_sem.at[2]),
    ]
    for c in smalls + weights:
        c.start()

    barrier = pltpu.get_barrier_semaphore()
    for o in OFFSETS:
        pl.semaphore_signal(barrier, inc=1, device_id=(peer(o), k), device_id_type=MESH)
    for i in range(1, NKV):
        pl.semaphore_signal(barrier, inc=1, device_id=(r, kv_peer(i)), device_id_type=MESH)

    k_copies = [pltpu.make_async_copy(kc.at[j, 0], k_s.at[j], k_sem.at[j]) for j in range(OWN)]
    v_copies = [pltpu.make_async_copy(vc.at[j, 0], v_s.at[j], v_sem.at[j]) for j in range(OWN)]
    wo_copy = pltpu.make_async_copy(wo, wo_s, w_sem.at[3])
    for c in k_copies + v_copies + [wo_copy]:
        c.start()

    slot = lax.broadcasted_iota(jnp.int32, (8, CYCLE), 1)
    lane = lax.broadcasted_iota(jnp.int32, (8, HD), 1)
    row = lax.broadcasted_iota(jnp.int32, (8, HD), 0)
    upper = row < 4
    pos = jnp.zeros((8, HD), jnp.float32)
    for j in range(OWN):
        length = lens[j]
        floor_at = jnp.maximum(sinks[j], length - wins[j])
        place = slot + CYCLE * jnp.right_shift(length - 1 - slot, 12)
        live = (slot < length) & (place >= floor_at)
        mask_s[j] = jnp.where(live, 0.0, -jnp.inf)
        elive = (lane < jnp.minimum(sinks[j], length)) | (lane == 4)
        emask_s[j] = jnp.where(elive, 0.0, -jnp.inf)
        pos = jnp.where(jnp.bitwise_and(row, 3) == j, length.astype(jnp.float32), pos)
    kext[...] = jnp.zeros_like(kext)
    vext[...] = jnp.zeros_like(vext)
    for c in smalls:
        c.wait()
    angle = pos * freq_s[...]
    cosine = jnp.cos(angle)
    sine = jnp.where(lane < HALF, -jnp.sin(angle), jnp.sin(angle))

    def line(v, c):
        return jnp.broadcast_to(v[c * HD : (c + 1) * HD].reshape(1, HD), (8, HD))

    bqv = bq_s[...].astype(jnp.float32)
    bkv = bk_s[...].astype(jnp.float32)
    bvv = bv_s[...].astype(jnp.float32)
    lines = [line(bqv, c) for c in range(GROUP)] + [line(bkv, 0), line(bvv, 0), jnp.zeros((8, HD), jnp.float32)]
    for t in range(4):
        bias_s[t] = jnp.where(upper, lines[2 * t], lines[2 * t + 1])
    pad4 = jnp.zeros((4, HD), jnp.float32)
    for j in range(OWN):
        sinkf_s[0, j] = jnp.concatenate([sk_s[j, 0].astype(jnp.float32), pad4], 0)
        sinkf_s[1, j] = jnp.concatenate([sv_s[j, 0].astype(jnp.float32), pad4], 0)
    gain_row = gain_s[...].astype(jnp.float32).reshape(1, FEAT)
    hid_copy.wait()

    pl.semaphore_wait(barrier, len(OFFSETS) + NKV - 1)

    def hid_send(i):
        return pltpu.make_async_remote_copy(
            hidall.at[k], hidall.at[k], s1.at[i - 1], r1.at[k], device_id=(r, kv_peer(i)), device_id_type=MESH
        )

    for i in range(1, NKV):
        hid_send(i).start()
    for c in weights:
        c.wait()
    for i in range(1, NKV):
        src = kv_peer(i)
        pltpu.make_async_remote_copy(
            hidall.at[src], hidall.at[src], s1.at[i - 1], r1.at[src], device_id=(r, src), device_id_type=MESH
        ).wait_recv()

    xf = hidall[...].astype(jnp.float32).reshape(NREQ * OWN, FEAT)
    squares = jnp.sum(xf * xf, axis=1, keepdims=True)
    scaled = (xf * gain_row).astype(jnp.bfloat16)
    part = jnp.dot(scaled, w_s[...], preferred_element_type=jnp.float32)
    for c in range(GROUP + 2):
        pb[c] = part[:, c * HD : (c + 1) * HD].astype(jnp.bfloat16)
    high = squares.astype(jnp.bfloat16).astype(jnp.float32)
    lane_all = lax.broadcasted_iota(jnp.int32, (NREQ * OWN, HD), 1)
    pb[GROUP + 2] = jnp.where(lane_all < HALF, high, squares - high).astype(jnp.bfloat16)

    def part_send(n, o):
        d = peer(o)
        return pltpu.make_async_remote_copy(
            pb.at[:, pl.ds(pl.multiple_of(d * OWN, OWN), OWN)],
            rb.at[r],
            s2.at[n],
            r2.at[r],
            device_id=(d, k),
            device_id_type=MESH,
        )

    for n, o in enumerate(OFFSETS):
        part_send(n, o).start()
    own_part = pltpu.make_async_copy(
        pb.at[:, pl.ds(pl.multiple_of(r * OWN, OWN), OWN)], rb.at[r], own_sem.at[1]
    )
    own_part.start()
    own_part.wait()
    for n, o in enumerate(OFFSETS):
        src = peer(o)
        pltpu.make_async_remote_copy(
            rb.at[src], rb.at[src], s2.at[n], r2.at[src], device_id=(src, k), device_id_type=MESH
        ).wait_recv()
    acc = rb[0].astype(jnp.float32)
    for i in range(1, NREQ):
        acc = acc + rb[i].astype(jnp.float32)
    acc = acc.reshape(4, 8, HD)

    tail = acc[3]
    tail = tail + pltpu.roll(tail, HALF, 1)
    tail = jnp.where(upper, pltpu.roll(tail, 4, 0), tail)
    inv_rms = lax.rsqrt(tail / D + 1e-6)
    full = acc * inv_rms[None] + bias_s[...]
    for t in range(3):
        qs[pl.ds(8 * t, 8), :] = full[t] * cosine + pltpu.roll(full[t], HALF, 1) * sine
    qs[pl.ds(24, 8), :] = full[3]

    scale = 1.0 / math.sqrt(HD)
    zeros8 = jnp.zeros((8, HD), jnp.float32)
    for j in range(OWN):
        heads = qs[pl.ds(j, 8, stride=4), :]
        qj = heads.astype(jnp.bfloat16)
        new_key = jnp.where(row == 4, jnp.broadcast_to(heads[5:6], (8, HD)), sinkf_s[0, j])
        new_value = jnp.where(row == 4, jnp.broadcast_to(heads[6:7], (8, HD)), sinkf_s[1, j])
        kext[j, pl.ds(0, 16), :] = jnp.concatenate([new_key, zeros8], 0).astype(jnp.bfloat16)
        vext[j, pl.ds(0, 16), :] = jnp.concatenate([new_value, zeros8], 0).astype(jnp.bfloat16)
        k_copies[j].wait()
        score = lax.dot_general(qj, k_s[j], NT, preferred_element_type=jnp.float32) * scale + mask_s[j]
        extra = lax.dot_general(qj, kext[j], NT, preferred_element_type=jnp.float32) * scale + emask_s[j]
        top = jnp.maximum(jnp.max(score, 1, keepdims=True), jnp.max(extra, 1, keepdims=True))
        weight = jnp.exp(score - top)
        eweight = jnp.exp(extra - top)
        total = jnp.sum(weight, 1, keepdims=True) + jnp.sum(eweight, 1, keepdims=True)
        v_copies[j].wait()
        numer = jnp.dot(weight.astype(jnp.bfloat16), v_s[j], preferred_element_type=jnp.float32)
        numer = numer + jnp.dot(eweight.astype(jnp.bfloat16), vext[j], preferred_element_type=jnp.float32)
        cs[pl.ds(j, 8, stride=4), :] = numer / total
    cb[...] = cs[...].astype(jnp.bfloat16).reshape(8, OWN, HD)

    mine = pl.ds(pl.multiple_of(r * OWN, OWN), OWN)

    def ctx_send(n, o):
        return pltpu.make_async_remote_copy(
            cb.at[pl.ds(0, GROUP)],
            rb2.at[:, mine],
            s4.at[n],
            r4.at[r],
            device_id=(peer(o), k),
            device_id_type=MESH,
        )

    for n, o in enumerate(OFFSETS):
        ctx_send(n, o).start()
    own_ctx = pltpu.make_async_copy(cb.at[pl.ds(0, GROUP)], rb2.at[:, mine], own_sem.at[2])
    own_ctx.start()
    own_ctx.wait()
    wo_copy.wait()
    for n, o in enumerate(OFFSETS):
        src = peer(o)
        theirs = pl.ds(pl.multiple_of(src * OWN, OWN), OWN)
        pltpu.make_async_remote_copy(
            cb.at[pl.ds(0, GROUP)], rb2.at[:, theirs], s4.at[n], r4.at[src], device_id=(src, k), device_id_type=MESH
        ).wait_recv()

    total_out = lax.dot_general(rb2[0], wo_s[:, 0:HD], NT, preferred_element_type=jnp.float32)
    for g in range(1, GROUP):
        total_out = total_out + lax.dot_general(
            rb2[g], wo_s[:, g * HD : (g + 1) * HD], NT, preferred_element_type=jnp.float32
        )
    yb[...] = total_out.reshape(NKV, ROWS, FEAT)

    def out_send(i):
        d = kv_peer(i)
        return pltpu.make_async_remote_copy(
            yb.at[d], rb3.at[k], s5.at[i - 1], r5.at[k], device_id=(r, d), device_id_type=MESH
        )

    for i in range(1, NKV):
        out_send(i).start()
    result = yb[k]
    for i in range(1, NKV):
        src = kv_peer(i)
        pltpu.make_async_remote_copy(
            rb3.at[src], rb3.at[src], s5.at[i - 1], r5.at[src], device_id=(r, src), device_id_type=MESH
        ).wait_recv()
        result = result + rb3[src]
    out[...] = result.astype(jnp.bfloat16)

    for i in range(1, NKV):
        hid_send(i).wait_send()
        out_send(i).wait_send()
    for n, o in enumerate(OFFSETS):
        part_send(n, o).wait_send()
        ctx_send(n, o).wait_send()


def on_device(
    hidden, gain, w_query, w_key, w_value, b_query, b_key, b_value, w_output,
    key_cache, value_cache, sink_keys, sink_values, lengths, sink_count, window,
):
    table = np.power(1000000.0, -2.0 * np.arange(HALF) / HD)
    freq = jnp.asarray(np.broadcast_to(np.concatenate([table, table]), (8, HD)), jnp.float32)
    anywhere = pl.BlockSpec(memory_space=pl.ANY)
    scalars = pl.BlockSpec(memory_space=pltpu.SMEM)
    bf, f32 = jnp.bfloat16, jnp.float32
    dma = pltpu.SemaphoreType.DMA
    return pl.pallas_call(
        kernel,
        out_shape=jax.ShapeDtypeStruct((ROWS, FEAT), bf),
        in_specs=[anywhere] * 14 + [scalars] * 3,
        out_specs=pl.BlockSpec(memory_space=pltpu.VMEM),
        scratch_shapes=[
            pltpu.VMEM((NKV, ROWS, FEAT), bf),
            pltpu.VMEM((FEAT,), bf),
            pltpu.VMEM((FEAT, QCOLS + 2 * HD), bf),
            pltpu.VMEM((QCOLS,), bf),
            pltpu.VMEM((HD,), bf),
            pltpu.VMEM((HD,), bf),
            pltpu.VMEM((FEAT, QCOLS), bf),
            pltpu.VMEM((OWN, CYCLE, HD), bf),
            pltpu.VMEM((OWN, CYCLE, HD), bf),
            pltpu.VMEM((OWN, 1, 4, HD), bf),
            pltpu.VMEM((OWN, 1, 4, HD), bf),
            pltpu.VMEM((8, HD), f32),
            pltpu.VMEM((OWN, 8, CYCLE), f32),
            pltpu.VMEM((OWN, 8, HD), f32),
            pltpu.VMEM((2, OWN, 8, HD), f32),
            pltpu.VMEM((4, 8, HD), f32),
            pltpu.VMEM((OWN, HD, HD), bf),
            pltpu.VMEM((OWN, HD, HD), bf),
            pltpu.VMEM((32, HD), f32),
            pltpu.VMEM((32, HD), f32),
            pltpu.VMEM((8, OWN, HD), bf),
            pltpu.VMEM((8, NREQ * OWN, HD), bf),
            pltpu.VMEM((NREQ, 8, OWN, HD), bf),
            pltpu.VMEM((GROUP, NREQ * OWN, HD), bf),
            pltpu.VMEM((NKV, ROWS, FEAT), f32),
            pltpu.VMEM((NKV, ROWS, FEAT), f32),
            dma((7,)), dma((4,)), dma((OWN,)), dma((OWN,)), dma((3,)),
            dma((NKV - 1,)), dma((NKV,)),
            dma((NREQ - 1,)), dma((NREQ,)),
            dma((NREQ - 1,)), dma((NREQ,)),
            dma((NKV - 1,)), dma((NKV,)),
        ],
        compiler_params=pltpu.CompilerParams(
            collective_id=0, has_side_effects=True, vmem_limit_bytes=60 * 1024 * 1024
        ),
    )(
        hidden, gain, w_query, w_key, w_value, b_query, b_key, b_value, w_output.T,
        key_cache, value_cache, sink_keys, sink_values, freq, lengths, sink_count, window,
    )


def solution(mesh):
    in_specs = (
        P("kv", "req"),
        P("req"),
        P("req", "kv"),
        P("req", "kv"),
        P("req", "kv"),
        P("kv"),
        P("kv"),
        P("kv"),
        P("kv", "req"),
        P("req", "kv", None, None),
        P("req", "kv", None, None),
        P("req", "kv", None, None),
        P("req", "kv", None, None),
        P("req"),
        P("req"),
        P("req"),
    )
    out_specs = P("kv", "req")

    def run(*args):
        with jax.sharding.use_abstract_mesh(mesh.abstract_mesh):
            return jax.shard_map(
                on_device, mesh=mesh, in_specs=in_specs, out_specs=out_specs, check_vma=False
            )(*args)

    return run
```

```python
import math

import jax
import jax.numpy as jnp
import numpy as np
from jax import lax
from jax.experimental import pallas as pl
from jax.experimental.pallas import tpu as pltpu
from jax.sharding import PartitionSpec as P

D = 5120
CYCLE = 4096
HD = 128
HALF = 64
GROUP = 5
NX, NZ = 4, 8
NREQ, NKV = 32, 8
OWN = 4
ROWS = 16
FEAT = 160
WIDE = 256
QCOLS = GROUP * HD
MESH = pl.DeviceIdType.MESH
OFFSETS = sorted(
    ((dx, dz) for dx in range(NX) for dz in range(NZ) if (dx, dz) != (0, 0)),
    key=lambda o: -(min(o[0], NX - o[0]) + min(o[1], NZ - o[1])),
)
NEAR = [(1, 0), (2, 0), (3, 0)]
ALONG = [(0, 1), (0, 7), (0, 2), (0, 6)]
NT = (((1,), (1,)), ((), ()))


def kernel(
    hid, gain, wq, wk, wv, bq, bk, bv, wo, kc, vc, sk, sv, freq, lens, sinks, wins,
    out,
    hid_s, hidall, gain_s, w_s, bq_s, bk_s, bv_s, wo_s, k_s, v_s, sk_s, sv_s, freq_s,
    mask_s, emask_s, sinkf_s, bias_s, kext, vext, qs, cs, cb,
    pb, rb, rb2, yf, yb, rb3,
    small_sem, w_sem, k_sem, v_sem, own_sem,
    round2, round3,
    s1, r1, s2, r2, s4, r4, s5, r5,
):
    r = lax.axis_index("req")
    k = lax.axis_index("kv")
    x, z = r // NZ, lax.rem(r, NZ)

    def peer(o):
        return lax.rem(x + o[0], NX) * NZ + lax.rem(z + o[1], NZ)

    def kv_peer(i):
        return lax.rem(k + i, NKV)

    hid_copy = pltpu.make_async_copy(hid, hid_s, own_sem.at[0])
    hid_copy.start()
    smalls = [
        pltpu.make_async_copy(a, b, small_sem.at[i])
        for i, (a, b) in enumerate(
            [(gain, gain_s), (bq, bq_s), (bk, bk_s), (bv, bv_s), (sk, sk_s), (sv, sv_s), (freq, freq_s)]
        )
    ]
    weights = [
        pltpu.make_async_copy(wq, w_s.at[:, pl.ds(0, QCOLS)], w_sem.at[0]),
        pltpu.make_async_copy(wk, w_s.at[:, pl.ds(QCOLS, HD)], w_sem.at[1]),
        pltpu.make_async_copy(wv, w_s.at[:, pl.ds(QCOLS + HD, HD)], w_sem.at[2]),
    ]
    for c in smalls + weights:
        c.start()

    def signal(sem, o):
        pl.semaphore_signal(sem, inc=1, device_id=(peer(o), k), device_id_type=MESH)

    barrier = pltpu.get_barrier_semaphore()
    for i in range(1, NKV):
        pl.semaphore_signal(barrier, inc=1, device_id=(r, kv_peer(i)), device_id_type=MESH)
    for o in NEAR + ALONG:
        signal(barrier, o)

    k_copies = [pltpu.make_async_copy(kc.at[j, 0], k_s.at[j], k_sem.at[j]) for j in range(OWN)]
    v_copies = [pltpu.make_async_copy(vc.at[j, 0], v_s.at[j], v_sem.at[j]) for j in range(OWN)]
    wo_copy = pltpu.make_async_copy(wo, wo_s, w_sem.at[3])
    for c in k_copies + v_copies + [wo_copy]:
        c.start()

    hid_copy.wait()
    hidall[k, :, 0:FEAT] = hid_s[...]

    pl.semaphore_wait(barrier, NKV - 1 + len(NEAR) + len(ALONG))

    def hid_send(i):
        return pltpu.make_async_remote_copy(
            hidall.at[k], hidall.at[k], s1.at[i - 1], r1.at[k], device_id=(r, kv_peer(i)), device_id_type=MESH
        )

    for i in range(1, NKV):
        hid_send(i).start()

    for o in ALONG:
        signal(round2, o)
    pl.semaphore_wait(round2, len(ALONG))
    for o in ALONG[2:]:
        signal(round3, o)

    for c in smalls:
        c.wait()
    for c in weights:
        c.wait()
    gain_row = gain_s[...].astype(jnp.float32).reshape(1, FEAT)
    for i in range(1, NKV):
        src = kv_peer(i)
        pltpu.make_async_remote_copy(
            hidall.at[src], hidall.at[src], s1.at[i - 1], r1.at[src], device_id=(r, src), device_id_type=MESH
        ).wait_recv()

    xf = hidall[:, :, 0:FEAT].astype(jnp.float32).reshape(NREQ * OWN, FEAT)
    squares = jnp.sum(xf * xf, axis=1, keepdims=True)
    scaled = (xf * gain_row).astype(jnp.bfloat16)
    part = jnp.dot(scaled, w_s[...], preferred_element_type=jnp.float32)
    for c in range(GROUP + 2):
        pb[c] = part[:, c * HD : (c + 1) * HD].astype(jnp.bfloat16)
    high = squares.astype(jnp.bfloat16).astype(jnp.float32)
    lane_all = lax.broadcasted_iota(jnp.int32, (NREQ * OWN, HD), 1)
    pb[GROUP + 2] = jnp.where(lane_all < HALF, high, squares - high).astype(jnp.bfloat16)

    def part_send(n, o):
        d = peer(o)
        return pltpu.make_async_remote_copy(
            pb.at[:, pl.ds(pl.multiple_of(d * OWN, OWN), OWN)],
            rb.at[r],
            s2.at[n],
            r2.at[r],
            device_id=(d, k),
            device_id_type=MESH,
        )

    pl.semaphore_wait(round3, len(ALONG) - 2)
    for n, o in enumerate(OFFSETS):
        part_send(n, o).start()
    own_part = pltpu.make_async_copy(
        pb.at[:, pl.ds(pl.multiple_of(r * OWN, OWN), OWN)], rb.at[r], own_sem.at[1]
    )
    own_part.start()

    slot = lax.broadcasted_iota(jnp.int32, (8, CYCLE), 1)
    lane = lax.broadcasted_iota(jnp.int32, (8, HD), 1)
    row = lax.broadcasted_iota(jnp.int32, (8, HD), 0)
    upper = row < 4
    pos = jnp.zeros((8, HD), jnp.float32)
    for j in range(OWN):
        length = lens[j]
        floor_at = jnp.maximum(sinks[j], length - wins[j])
        place = slot + CYCLE * jnp.right_shift(length - 1 - slot, 12)
        live = (slot < length) & (place >= floor_at)
        mask_s[j] = jnp.where(live, 0.0, -jnp.inf)
        elive = (lane < jnp.minimum(sinks[j], length)) | (lane == 4)
        emask_s[j] = jnp.where(elive, 0.0, -jnp.inf)
        pos = jnp.where(jnp.bitwise_and(row, 3) == j, length.astype(jnp.float32), pos)
    kext[...] = jnp.zeros_like(kext)
    vext[...] = jnp.zeros_like(vext)
    angle = pos * freq_s[...]
    cosine = jnp.cos(angle)
    sine = jnp.where(lane < HALF, -jnp.sin(angle), jnp.sin(angle))

    def line(v, c):
        return jnp.broadcast_to(v[c * HD : (c + 1) * HD].reshape(1, HD), (8, HD))

    bqv = bq_s[...].astype(jnp.float32)
    bkv = bk_s[...].astype(jnp.float32)
    bvv = bv_s[...].astype(jnp.float32)
    lines = [line(bqv, c) for c in range(GROUP)] + [line(bkv, 0), line(bvv, 0), jnp.zeros((8, HD), jnp.float32)]
    for t in range(4):
        bias_s[t] = jnp.where(upper, lines[2 * t], lines[2 * t + 1])
    pad4 = jnp.zeros((4, HD), jnp.float32)
    for j in range(OWN):
        sinkf_s[0, j] = jnp.concatenate([sk_s[j, 0].astype(jnp.float32), pad4], 0)
        sinkf_s[1, j] = jnp.concatenate([sv_s[j, 0].astype(jnp.float32), pad4], 0)
    own_part.wait()
    for n, o in enumerate(OFFSETS):
        src = peer(o)
        pltpu.make_async_remote_copy(
            rb.at[src], rb.at[src], s2.at[n], r2.at[src], device_id=(src, k), device_id_type=MESH
        ).wait_recv()
    acc = rb[0].astype(jnp.float32)
    for i in range(1, NREQ):
        acc = acc + rb[i].astype(jnp.float32)
    acc = acc.reshape(4, 8, HD)

    tail = acc[3]
    tail = tail + pltpu.roll(tail, HALF, 1)
    tail = jnp.where(upper, pltpu.roll(tail, 4, 0), tail)
    inv_rms = lax.rsqrt(tail / D + 1e-6)
    full = acc * inv_rms[None] + bias_s[...]
    for t in range(3):
        qs[pl.ds(8 * t, 8), :] = full[t] * cosine + pltpu.roll(full[t], HALF, 1) * sine
    qs[pl.ds(24, 8), :] = full[3]

    scale = 1.0 / math.sqrt(HD)
    zeros8 = jnp.zeros((8, HD), jnp.float32)
    for j in range(OWN):
        heads = qs[pl.ds(j, 8, stride=4), :]
        qj = heads.astype(jnp.bfloat16)
        new_key = jnp.where(row == 4, jnp.broadcast_to(heads[5:6], (8, HD)), sinkf_s[0, j])
        new_value = jnp.where(row == 4, jnp.broadcast_to(heads[6:7], (8, HD)), sinkf_s[1, j])
        kext[j, pl.ds(0, 16), :] = jnp.concatenate([new_key, zeros8], 0).astype(jnp.bfloat16)
        vext[j, pl.ds(0, 16), :] = jnp.concatenate([new_value, zeros8], 0).astype(jnp.bfloat16)
        k_copies[j].wait()
        score = lax.dot_general(qj, k_s[j], NT, preferred_element_type=jnp.float32) * scale + mask_s[j]
        extra = lax.dot_general(qj, kext[j], NT, preferred_element_type=jnp.float32) * scale + emask_s[j]
        top = jnp.maximum(jnp.max(score, 1, keepdims=True), jnp.max(extra, 1, keepdims=True))
        weight = jnp.exp(score - top)
        eweight = jnp.exp(extra - top)
        total = jnp.sum(weight, 1, keepdims=True) + jnp.sum(eweight, 1, keepdims=True)
        v_copies[j].wait()
        numer = jnp.dot(weight.astype(jnp.bfloat16), v_s[j], preferred_element_type=jnp.float32)
        numer = numer + jnp.dot(eweight.astype(jnp.bfloat16), vext[j], preferred_element_type=jnp.float32)
        cs[pl.ds(j, 8, stride=4), :] = numer / total
    cb[...] = cs[...].astype(jnp.bfloat16).reshape(8, OWN, HD)

    mine = pl.ds(pl.multiple_of(r * OWN, OWN), OWN)

    def ctx_send(n, o):
        return pltpu.make_async_remote_copy(
            cb.at[pl.ds(0, GROUP)],
            rb2.at[:, mine],
            s4.at[n],
            r4.at[r],
            device_id=(peer(o), k),
            device_id_type=MESH,
        )

    for n, o in enumerate(OFFSETS):
        ctx_send(n, o).start()
    own_ctx = pltpu.make_async_copy(cb.at[pl.ds(0, GROUP)], rb2.at[:, mine], own_sem.at[2])
    own_ctx.start()
    own_ctx.wait()
    wo_copy.wait()
    for n, o in enumerate(OFFSETS):
        src = peer(o)
        theirs = pl.ds(pl.multiple_of(src * OWN, OWN), OWN)
        pltpu.make_async_remote_copy(
            cb.at[pl.ds(0, GROUP)], rb2.at[:, theirs], s4.at[n], r4.at[src], device_id=(src, k), device_id_type=MESH
        ).wait_recv()

    total_out = lax.dot_general(rb2[0], wo_s[:, 0:HD], NT, preferred_element_type=jnp.float32)
    for g in range(1, GROUP):
        total_out = total_out + lax.dot_general(
            rb2[g], wo_s[:, g * HD : (g + 1) * HD], NT, preferred_element_type=jnp.float32
        )
    total_out = total_out.reshape(NKV, ROWS, FEAT)
    yf[...] = total_out
    yb[:, :, 0:FEAT] = total_out.astype(jnp.bfloat16)

    def out_send(i):
        d = kv_peer(i)
        return pltpu.make_async_remote_copy(
            yb.at[d], rb3.at[k], s5.at[i - 1], r5.at[k], device_id=(r, d), device_id_type=MESH
        )

    for i in range(1, NKV):
        out_send(i).start()
    result = yf[k]
    for i in range(1, NKV):
        src = kv_peer(i)
        pltpu.make_async_remote_copy(
            rb3.at[src], rb3.at[src], s5.at[i - 1], r5.at[src], device_id=(r, src), device_id_type=MESH
        ).wait_recv()
        result = result + rb3[src, :, 0:FEAT].astype(jnp.float32)
    out[...] = result.astype(jnp.bfloat16)

    for i in range(1, NKV):
        hid_send(i).wait_send()
        out_send(i).wait_send()
    for n, o in enumerate(OFFSETS):
        part_send(n, o).wait_send()
        ctx_send(n, o).wait_send()


def on_device(
    hidden, gain, w_query, w_key, w_value, b_query, b_key, b_value, w_output,
    key_cache, value_cache, sink_keys, sink_values, lengths, sink_count, window,
):
    table = np.power(1000000.0, -2.0 * np.arange(HALF) / HD)
    freq = jnp.asarray(np.broadcast_to(np.concatenate([table, table]), (8, HD)), jnp.float32)
    anywhere = pl.BlockSpec(memory_space=pl.ANY)
    scalars = pl.BlockSpec(memory_space=pltpu.SMEM)
    bf, f32 = jnp.bfloat16, jnp.float32
    dma = pltpu.SemaphoreType.DMA
    return pl.pallas_call(
        kernel,
        out_shape=pltpu.VMEM((ROWS, FEAT), bf),
        in_specs=[anywhere] * 14 + [scalars] * 3,
        out_specs=pl.BlockSpec(memory_space=pltpu.VMEM),
        scratch_shapes=[
            pltpu.VMEM((ROWS, FEAT), bf),
            pltpu.VMEM((NKV, ROWS, WIDE), bf),
            pltpu.VMEM((FEAT,), bf),
            pltpu.VMEM((FEAT, QCOLS + 2 * HD), bf),
            pltpu.VMEM((QCOLS,), bf),
            pltpu.VMEM((HD,), bf),
            pltpu.VMEM((HD,), bf),
            pltpu.VMEM((FEAT, QCOLS), bf),
            pltpu.VMEM((OWN, CYCLE, HD), bf),
            pltpu.VMEM((OWN, CYCLE, HD), bf),
            pltpu.VMEM((OWN, 1, 4, HD), bf),
            pltpu.VMEM((OWN, 1, 4, HD), bf),
            pltpu.VMEM((8, HD), f32),
            pltpu.VMEM((OWN, 8, CYCLE), f32),
            pltpu.VMEM((OWN, 8, HD), f32),
            pltpu.VMEM((2, OWN, 8, HD), f32),
            pltpu.VMEM((4, 8, HD), f32),
            pltpu.VMEM((OWN, HD, HD), bf),
            pltpu.VMEM((OWN, HD, HD), bf),
            pltpu.VMEM((32, HD), f32),
            pltpu.VMEM((32, HD), f32),
            pltpu.VMEM((8, OWN, HD), bf),
            pltpu.VMEM((8, NREQ * OWN, HD), bf),
            pltpu.VMEM((NREQ, 8, OWN, HD), bf),
            pltpu.VMEM((GROUP, NREQ * OWN, HD), bf),
            pltpu.VMEM((NKV, ROWS, FEAT), f32),
            pltpu.VMEM((NKV, ROWS, WIDE), bf),
            pltpu.VMEM((NKV, ROWS, WIDE), bf),
            dma((7,)), dma((4,)), dma((OWN,)), dma((OWN,)), dma((3,)),
            pltpu.SemaphoreType.REGULAR, pltpu.SemaphoreType.REGULAR,
            dma((NKV - 1,)), dma((NKV,)),
            dma((NREQ - 1,)), dma((NREQ,)),
            dma((NREQ - 1,)), dma((NREQ,)),
            dma((NKV - 1,)), dma((NKV,)),
        ],
        compiler_params=pltpu.CompilerParams(
            collective_id=0, has_side_effects=True, vmem_limit_bytes=60 * 1024 * 1024
        ),
    )(
        hidden, gain, w_query, w_key, w_value, b_query, b_key, b_value, w_output.T,
        key_cache, value_cache, sink_keys, sink_values, freq, lengths, sink_count, window,
    )


def solution(mesh):
    in_specs = (
        P("kv", "req"),
        P("req"),
        P("req", "kv"),
        P("req", "kv"),
        P("req", "kv"),
        P("kv"),
        P("kv"),
        P("kv"),
        P("kv", "req"),
        P("req", "kv", None, None),
        P("req", "kv", None, None),
        P("req", "kv", None, None),
        P("req", "kv", None, None),
        P("req"),
        P("req"),
        P("req"),
    )
    out_specs = P("kv", "req")

    def run(*args):
        with jax.sharding.use_abstract_mesh(mesh.abstract_mesh):
            return jax.shard_map(
                on_device, mesh=mesh, in_specs=in_specs, out_specs=out_specs, check_vma=False
            )(*args)

    return run
```
